512 devices in a mesh: sec: 32 (over z, x), op: 16 (over y, core).
Axes of the slice: x: 4, y: 8, z: 8, core: 2. Of those that a mesh axis runs over, the one named last changes fastest.
Arguments:
- state: float32 [32, 256, 256], P('sec'), may hold values from -6 to 6
- left_ops: float32 [128, 32, 256, 256], P('op', 'sec'), may hold values from -0.03125 to 0.03125
- right_ops: float32 [128, 32, 256, 256], P('op', 'sec'), may hold values from -0.375 to 0.375
- term_shift: int32 [128], P('op'), may hold values from -1 to 1
- sector_rows: int32 [32], P('sec'), may hold values from 128 to 256, as said below
- sector_cols: int32 [32], P('sec'), may hold values from 128 to 256, as said below
Outputs:
- correction: float32 [32, 256, 256], P('sec')
- image: float32 [32, 256, 256], P('sec')
The draws below stay inside these ranges and needn't reach their ends.
Inputs may be any that keep to these rules, and one draw needn't show every extreme that they name: `sector_rows`: at least one sector has 256 live rows. `sector_cols`: at least one sector has 256 live columns.
All inputs are finite; a program needn't handle non-finite values.
Results may differ from the reference program's by a relative error of at most 0.0003.
Values sent between devices are 32-bit elements; how exact they have to be, the bound alone decides.
A program may use at most 64 MiB of HBM per device.

```python
import jax
import jax.numpy as jnp
from jax import lax

BLOCK = 256
SECTORS = 32
TERMS = 128


def live_counts(key):
    values = jax.random.randint(key, (SECTORS,), BLOCK // 2, BLOCK + 1)
    where_full = jax.random.randint(jax.random.fold_in(key, 7), (), 0, SECTORS)
    place = jnp.arange(SECTORS, dtype=jnp.int32)
    return jnp.where(place == where_full, BLOCK, values).astype(jnp.int32)


def draw_sector_rows(key, part):
    return live_counts(jax.random.fold_in(key, 11))


def draw_sector_cols(key, part):
    return live_counts(jax.random.fold_in(key, 23))


def with_ends(values, own_key, low, high):
    spot = [jax.random.randint(jax.random.fold_in(own_key, axis), (), 0, length) for axis, length in enumerate(values.shape)]
    longest = values.shape.index(max(values.shape))
    next_to = spot[:longest] + [(spot[longest] + 1) % values.shape[longest]] + spot[longest + 1:]
    return values.at[tuple(spot)].set(low).at[tuple(next_to)].set(high)


def level_of(stream_key, extent, shards, smallest, largest):
    def one(axis_at, blocks):
        draws = jax.random.uniform(jax.random.fold_in(jax.random.fold_in(stream_key, 6), axis_at), (blocks,), jnp.float32, smallest / len(shards), largest / len(shards))
        return jnp.repeat(jnp.exp(draws), extent[axis_at] // blocks).reshape((-1,) + (1,) * (len(extent) - axis_at - 1))

    gain = one(*shards[0])
    for cut in shards[1:]:
        gain = gain * one(*cut)
    return gain


def bell_draw(key, shape, deviation, reach, cuts=(), kind=jnp.bfloat16):
    values = deviation * jax.random.normal(key, shape, jnp.float32)
    if cuts:
        values = values * level_of(key, shape, cuts, -0.22, 0.18)
    return jnp.clip(values, -reach, reach).astype(kind)


def setup_inputs(seed: int = 0) -> dict:
    streams_of = jax.random.split(jax.random.key(seed), 7)
    return {
        "state": bell_draw(streams_of[0], (SECTORS, BLOCK, BLOCK), 1.0, 6.0, ((0, 32),), jnp.float32),
        "left_ops": bell_draw(streams_of[1], (TERMS, SECTORS, BLOCK, BLOCK), (BLOCK * TERMS) ** -0.5, 0.03125, ((0, 16), (1, 32)), jnp.float32),
        "right_ops": bell_draw(streams_of[2], (TERMS, SECTORS, BLOCK, BLOCK), BLOCK ** -0.5, 0.375, ((0, 16), (1, 32)), jnp.float32),
        "term_shift": with_ends(jax.random.randint(streams_of[3], (TERMS,), -1, 2), jax.random.fold_in(streams_of[3], 1), -1, 1).astype(jnp.int32),
        "sector_rows": draw_sector_rows(jax.random.fold_in(streams_of[6], 71), 0),
        "sector_cols": draw_sector_cols(jax.random.fold_in(streams_of[6], 71), 0),
    }


def live_mask(sector_rows, sector_cols, block):
    place = jnp.arange(block, dtype=jnp.int32)
    rows_ok = place[None, :, None] < sector_rows[:, None, None]
    cols_ok = place[None, None, :] < sector_cols[:, None, None]
    return (rows_ok & cols_ok).astype(jnp.float32)

def hamiltonian(field, left_ops, right_ops, term_shift, mask):
    count = field.shape[0]
    padded = jnp.pad(field, ((1, 1), (0, 0), (0, 0)))

    def step(total, items):
        left, right, shift = items
        source = lax.dynamic_slice_in_dim(padded, (1 - shift).astype(jnp.int32), count, 0)
        inner = jnp.einsum('tij,tjl->til', left, source, precision=lax.Precision.HIGHEST)
        total = total + jnp.einsum('til,tml->tim', inner, right, precision=lax.Precision.HIGHEST)
        return (total, None)
    total, _ = lax.scan(step, jnp.zeros(field.shape, jnp.float32), (left_ops, right_ops, term_shift))
    return total * mask

def reference(state, left_ops, right_ops, term_shift, sector_rows, sector_cols):
    mask = live_mask(sector_rows, sector_cols, BLOCK)
    field = state * mask
    first = hamiltonian(field, left_ops, right_ops, term_shift, mask)
    theta = jnp.sum(field * first) / jnp.sum(field * field)
    resid = first - theta * field
    scale = lax.rsqrt(jnp.sum(resid * resid) / (SECTORS * BLOCK * BLOCK) + 1e-06)
    correction = resid * scale
    image = hamiltonian(correction, left_ops, right_ops, term_shift, mask)
    return (correction, image)
```

```python
import functools

import jax
import jax.numpy as jnp
from jax import lax
from jax.experimental import pallas as pl
from jax.experimental.pallas import tpu as pltpu
from jax.sharding import PartitionSpec as P

MESH = pl.DeviceIdType.MESH
SEC_X = 4
LANES = 128
NN = (((1,), (0,)), ((), ()))
NT = (((1,), (1,)), ((), ()))


def split(value):
    high = value.astype(jnp.bfloat16)
    return high, (value - high.astype(jnp.float32)).astype(jnp.bfloat16)


def dot(a, b, dims):
    return lax.dot_general(a, b, dims, preferred_element_type=jnp.float32)


def dot3(a_high, a_low, b_high, b_low, dims):
    return dot(a_high, b_high, dims) + (dot(a_low, b_high, dims) + dot(a_high, b_low, dims))


def kernel(
    sizes,
    state, left, right, shift, rows, cols,
    corr, image,
    state_v, left_f, right_f, shift_s, rows_s, cols_s,
    left_c, right_c, vec_c,
    field, near1, near2, part1, part2, sib1, sib2, sum1, sum2, box1, box2,
    full, full_i, scal_x, scal_z,
    local_sem, send_sem, recv_sem,
):
    n_sec, n_op, terms, block = sizes
    n_x = min(SEC_X, n_sec)
    n_z = n_sec // n_x
    n_y = n_op // 2
    piece = block // n_y
    s, o = lax.axis_index("sec"), lax.axis_index("op")
    y, c = o // 2, o % 2
    x, z = s % n_x, s // n_x
    mate = (s, y * 2 + (1 - c))
    after, before = ((s + 1) % n_sec, o), ((s + n_sec - 1) % n_sec, o)
    along_y = [(s, ((y + d) % n_y) * 2 + c) for d in range(1, n_y)]
    along_x = [(z * n_x + (x + d) % n_x, o) for d in range(1, n_x)]
    along_z = [(((z + d) % n_z) * n_x + x, o) for d in range(1, n_z)]

    count = [0]
    sent = []

    def remote(src, dst, device):
        i = count[0]
        count[0] += 1
        copy = pltpu.make_async_remote_copy(
            src_ref=src, dst_ref=dst, send_sem=send_sem.at[i], recv_sem=recv_sem.at[i],
            device_id=device, device_id_type=MESH,
        )
        copy.start()
        sent.append(copy)
        return copy

    partners = [mate, after, before] + along_y + along_x + along_z
    barrier = pltpu.get_barrier_semaphore()
    for device in partners:
        pl.semaphore_signal(barrier, inc=1, device_id=device, device_id_type=MESH)

    local = [
        pltpu.make_async_copy(src, dst, local_sem.at[i])
        for i, (src, dst) in enumerate(
            [(state.at[0], state_v), (rows, rows_s), (cols, cols_s), (shift, shift_s),
             (left.at[:, 0], left_f), (right.at[:, 0], right_f)]
        )
    ]
    for copy in local:
        copy.start()
    for copy in local[:3]:
        copy.wait()
    n_rows, n_cols = rows_s[0], cols_s[0]

    def masked(value, row0, col0):
        at_row = lax.broadcasted_iota(jnp.int32, value.shape, 0) + row0
        at_col = lax.broadcasted_iota(jnp.int32, value.shape, 1) + col0
        return value * ((at_row < n_rows) & (at_col < n_cols)).astype(jnp.float32)

    for h in range(2):
        field[h] = masked(state_v[:, h * LANES:(h + 1) * LANES], 0, h * LANES)
    pl.semaphore_wait(barrier, len(partners))

    def send_half(src, near):
        return [remote(src.at[c], near.at[0, c], after), remote(src.at[c], near.at[1, c], before)]

    def pass_on(copies, near):
        on = []
        for side in range(2):
            copies[side].wait_recv()
            on.append(remote(near.at[side, c], near.at[side, c], mate))
        return on

    def to_bf16(src, slot, keep=None):
        for h in range(2):
            value = src[h]
            if keep is not None:
                value = jnp.where(keep, value, 0.0)
            high, low = split(value)
            vec_c[slot, 0:block, h * LANES:(h + 1) * LANES] = high
            vec_c[slot, block:2 * block, h * LANES:(h + 1) * LANES] = low

    def product(part):
        total = None
        for k in range(terms):
            at = 1 - shift_s[k]
            inner = dot3(
                left_c[0, k], left_c[1, k], vec_c[at, 0:block], vec_c[at, block:2 * block], NN
            )
            high, low = split(inner)
            term = dot3(high, low, right_c[0, k], right_c[1, k], NT)
            total = term if total is None else total + term
        for h in range(2):
            part[h] = total[:, h * LANES:(h + 1) * LANES]

    mine = pl.ds(pl.multiple_of(y * piece, piece), piece)

    def scatter_sum(part, sib, summed, box, while_waiting=None):
        swap = remote(part.at[1 - c], sib, mate)
        if while_waiting is not None:
            while_waiting()
        swap.wait_recv()
        summed[...] = part[c] + sib[...]
        copies = []
        for d in range(1, n_y):
            to = (y + d) % n_y
            copies.append(
                remote(
                    summed.at[pl.ds(pl.multiple_of(to * piece, piece), piece)],
                    box.at[d], along_y[d - 1],
                )
            )
        total = summed[mine]
        for d in range(1, n_y):
            copies[d - 1].wait_recv()
            total = total + box[d]
        return masked(total, y * piece, c * LANES)

    def gather(whole):
        copies = [
            remote(whole.at[c, mine], whole.at[c, mine], along_y[d - 1]) for d in range(1, n_y)
        ]
        for copy in copies:
            copy.wait_recv()

    copies = send_half(field, near1)
    to_bf16(field, 1)
    for copy in local[3:]:
        copy.wait()
    for k in range(terms):
        left_c[0, k], left_c[1, k] = split(left_f[k])
        right_c[0, k], right_c[1, k] = split(right_f[k])
    for copy in pass_on(copies, near1):
        copy.wait_recv()
    to_bf16(near1.at[0], 0, s > 0)
    to_bf16(near1.at[1], 2, s < n_sec - 1)
    product(part1)
    full[c, mine] = scatter_sum(part1, sib1, sum1, box1)
    gather(full)

    own_half = remote(full.at[c], full.at[c], mate)
    copies = send_half(full, near2)
    own_half.wait_recv()
    to_bf16(full, 1)

    def total_of(terms_of):
        value = terms_of(0) + terms_of(1)
        return jnp.sum(jnp.sum(value, axis=0, keepdims=True), axis=1, keepdims=True)

    square = total_of(lambda h: field[h] * field[h])
    cross = total_of(lambda h: field[h] * full[h])
    own_theta = jnp.where(square > 0, cross / square, 0.0)
    rest = total_of(lambda h: (full[h] - own_theta * field[h]) * (full[h] - own_theta * field[h]))
    at = lax.broadcasted_iota(jnp.int32, (8, LANES), 0)
    scal_x[x] = jnp.where(at == 0, square, jnp.where(at == 1, cross, rest))
    x_copies = [remote(scal_x.at[x], scal_x.at[x], device) for device in along_x]

    for copy in pass_on(copies, near2):
        copy.wait_recv()
    to_bf16(near2.at[0], 0, s > 0)
    to_bf16(near2.at[1], 2, s < n_sec - 1)
    product(part2)
    z_copies = []

    def pass_scalars():
        for copy in x_copies:
            copy.wait_recv()
        scal_z[z] = scal_x[...]
        z_copies.extend(remote(scal_z.at[z], scal_z.at[z], device) for device in along_z)

    second = scatter_sum(part2, sib2, sum2, box2, pass_scalars)
    for copy in z_copies:
        copy.wait_recv()

    def all_of(i):
        return jnp.concatenate([scal_z[a, b, i:i + 1, :] for a in range(n_z) for b in range(n_x)], axis=0)

    squares, crosses, rests = all_of(0), all_of(1), all_of(2)
    thetas = jnp.where(squares > 0, crosses / squares, 0.0)
    theta = jnp.sum(crosses, axis=0, keepdims=True) / jnp.sum(squares, axis=0, keepdims=True)
    gap = (thetas - theta) * jnp.sqrt(squares)
    energy = jnp.sum(rests + gap * gap, axis=0, keepdims=True)
    scale = lax.rsqrt(energy / (n_sec * block * block) + 1e-06)

    full_i[c, mine] = scale * (second - theta * full[c, mine])
    gather(full_i)
    own_half = remote(full_i.at[c], full_i.at[c], mate)
    for h in range(2):
        corr[:, h * LANES:(h + 1) * LANES] = (full[h] - theta * field[h]) * scale
    own_half.wait_recv()
    for h in range(2):
        image[:, h * LANES:(h + 1) * LANES] = full_i[h]
    for copy in sent:
        copy.wait_send()


def local(n_sec, n_op, state, left, right, shift, rows, cols):
    terms, block = left.shape[0], state.shape[1]
    n_x = min(SEC_X, n_sec)
    n_y = n_op // 2
    piece = block // n_y
    f32, bf16 = jnp.float32, jnp.bfloat16
    n_copies = 64
    half = (block, LANES)
    corr, image = pl.pallas_call(
        functools.partial(kernel, (n_sec, n_op, terms, block)),
        out_shape=[jax.ShapeDtypeStruct((block, block), f32)] * 2,
        in_specs=[pl.BlockSpec(memory_space=pl.ANY)] * 6,
        out_specs=[pl.BlockSpec(memory_space=pltpu.VMEM)] * 2,
        scratch_shapes=[
            pltpu.VMEM((block, block), f32),
            pltpu.VMEM((terms, block, block), f32),
            pltpu.VMEM((terms, block, block), f32),
            pltpu.SMEM((terms,), jnp.int32),
            pltpu.SMEM((1,), jnp.int32),
            pltpu.SMEM((1,), jnp.int32),
            pltpu.VMEM((2, terms, block, block), bf16),
            pltpu.VMEM((2, terms, block, block), bf16),
            pltpu.VMEM((3, 2 * block, block), bf16),
            pltpu.VMEM((2,) + half, f32),
            pltpu.VMEM((2, 2) + half, f32),
            pltpu.VMEM((2, 2) + half, f32),
            pltpu.VMEM((2,) + half, f32),
            pltpu.VMEM((2,) + half, f32),
            pltpu.VMEM(half, f32),
            pltpu.VMEM(half, f32),
            pltpu.VMEM(half, f32),
            pltpu.VMEM(half, f32),
            pltpu.VMEM((n_y, piece, LANES), f32),
            pltpu.VMEM((n_y, piece, LANES), f32),
            pltpu.VMEM((2,) + half, f32),
            pltpu.VMEM((2,) + half, f32),
            pltpu.VMEM((n_x, 8, LANES), f32),
            pltpu.VMEM((n_sec // n_x, n_x, 8, LANES), f32),
            pltpu.SemaphoreType.DMA((6,)),
            pltpu.SemaphoreType.DMA((n_copies,)),
            pltpu.SemaphoreType.DMA((n_copies,)),
        ],
        compiler_params=pltpu.CompilerParams(
            collective_id=0, has_side_effects=True, vmem_limit_bytes=40 << 20
        ),
        name="davidson",
    )(state, left, right, shift, rows, cols)
    return corr[None], image[None]


def solution(mesh):
    in_specs = (
        P("sec", None, None),
        P("op", "sec", None, None),
        P("op", "sec", None, None),
        P("op"),
        P("sec"),
        P("sec"),
    )
    out_specs = (P("sec", None, None), P("sec", None, None))
    return jax.shard_map(
        functools.partial(local, mesh.shape["sec"], mesh.shape["op"]),
        mesh=mesh, in_specs=in_specs, out_specs=out_specs, check_vma=False,
    )
```

```python
import functools

import jax
import jax.numpy as jnp
from jax import lax
from jax.experimental import pallas as pl
from jax.experimental.pallas import tpu as pltpu
from jax.sharding import PartitionSpec as P

MESH = pl.DeviceIdType.MESH
SEC_X = 4
LANES = 128
NEAR_TO_FAR = ((0, 1, 7), (2, 6), (3, 5, 4))
FAR_FIRST = (4, 3, 5, 2, 6, 1, 7)
NN = (((1,), (0,)), ((), ()))
NT = (((1,), (1,)), ((), ()))


def split(value):
    high = value.astype(jnp.bfloat16)
    return high, (value - high.astype(jnp.float32)).astype(jnp.bfloat16)


def dot(a, b, dims):
    return lax.dot_general(a, b, dims, preferred_element_type=jnp.float32)


def dot3(a_high, a_low, b_high, b_low, dims):
    return dot(a_high, b_high, dims) + (dot(a_low, b_high, dims) + dot(a_high, b_low, dims))


def kernel(
    sizes,
    state, left, right, shift, rows, cols,
    corr, image,
    state_v, left_f, right_f, shift_s, rows_s, cols_s,
    left_c, right_c, vec_c,
    field, near1, near2, part1, part2, sib1, sib2, sum1, sum2, box1, box2,
    full, last, counts, near_counts, scal_x, scal_z,
    local_sem, send_sem, recv_sem,
):
    n_sec, n_op, terms, block = sizes
    n_x = min(SEC_X, n_sec)
    n_z = n_sec // n_x
    n_y = n_op // 2
    half = block // 2
    piece = half // n_y
    order = [d for group in NEAR_TO_FAR for d in group]
    at_slot = {d: i for i, d in enumerate(order)}
    s, o = lax.axis_index("sec"), lax.axis_index("op")
    y, c = o // 2, o % 2
    x, z = s % n_x, s // n_x
    mate = (s, y * 2 + (1 - c))
    after, before = ((s + 1) % n_sec, o), ((s + n_sec - 1) % n_sec, o)
    along_y = {d: (s, ((y + d) % n_y) * 2 + c) for d in FAR_FIRST}
    along_x = [(z * n_x + (x + d) % n_x, o) for d in range(1, n_x)]
    along_z = [(((z + d) % n_z) * n_x + x, o) for d in range(1, n_z)]

    count = [0]
    sent = []

    def remote(src, dst, device):
        i = count[0]
        count[0] += 1
        copy = pltpu.make_async_remote_copy(
            src_ref=src, dst_ref=dst, send_sem=send_sem.at[i], recv_sem=recv_sem.at[i],
            device_id=device, device_id_type=MESH,
        )
        copy.start()
        sent.append(copy)
        return copy

    def tile_rows(index, size):
        return pl.ds(pl.multiple_of(index * size, size), size)

    partners = [mate, after, before, *along_y.values(), *along_x, *along_z]
    barrier = pltpu.get_barrier_semaphore()
    for device in partners:
        pl.semaphore_signal(barrier, inc=1, device_id=device, device_id_type=MESH)

    def load(i, src, dst):
        copy = pltpu.make_async_copy(src, dst, local_sem.at[i])
        copy.start()
        return copy

    small = [load(0, rows, rows_s), load(1, cols, cols_s), load(2, shift, shift_s)]
    pl.semaphore_wait(barrier, len(partners))

    to_after = remote(state.at[0, tile_rows(c, half)], near1.at[0, c], after)
    to_before = remote(state.at[0, tile_rows(c, half)], near1.at[1, c], before)
    own_state = load(3, state.at[0], state_v)
    operators = [load(4, left.at[:, 0], left_f), load(5, right.at[:, 0], right_f)]
    for copy in small:
        copy.wait()
    n_rows, n_cols = rows_s[0], cols_s[0]
    at = lax.broadcasted_iota(jnp.int32, counts.shape, 0)
    counts[...] = jnp.where(at == 0, n_rows, n_cols)
    count_copies = [
        remote(counts, near_counts.at[0], after), remote(counts, near_counts.at[1], before)
    ]

    def masked(value, row0, some_rows, some_cols):
        at_row = lax.broadcasted_iota(jnp.int32, value.shape, 0) + row0
        at_col = lax.broadcasted_iota(jnp.int32, value.shape, 1)
        return value * ((at_row < some_rows) & (at_col < some_cols)).astype(jnp.float32)

    def hold(slot, where, value):
        high, low = split(value)
        vec_c[slot, 0, where] = high
        vec_c[slot, 1, where] = low

    def product(part):
        total = None
        for k in range(terms):
            source = 1 - shift_s[k]
            inner = dot3(left_c[0, k], left_c[1, k], vec_c[source, 0], vec_c[source, 1], NN)
            high, low = split(inner)
            term = dot3(high, low, right_c[0, k], right_c[1, k], NT)
            total = term if total is None else total + term
        part[0] = total[:half]
        part[1] = total[half:]

    def scatter_sum(part, sib, summed, box):
        swap = remote(part.at[1 - c], sib, mate)
        swap.wait_recv()
        summed[...] = part[c] + sib[...]
        copies = {}
        for d in FAR_FIRST:
            to = (y + d) % n_y
            copies[d] = remote(summed.at[tile_rows(to, piece)], box.at[d], along_y[d])
        total = summed[tile_rows(y, piece)]
        for d in order[1:]:
            copies[d].wait_recv()
            total = total + box[d]
        return masked(total, c * half + y * piece, n_rows, n_cols)

    def exist(side):
        return s > 0 if side == 0 else s < n_sec - 1

    own_state.wait()
    field[...] = masked(state_v[...], 0, n_rows, n_cols)
    hold(1, slice(None), field[...])
    for copy in operators:
        copy.wait()
    for k in range(terms):
        left_c[0, k], left_c[1, k] = split(left_f[k])
        right_c[0, k], right_c[1, k] = split(right_f[k])
    passed = []
    for side, copy in enumerate((to_after, to_before)):
        copy.wait_recv()
        passed.append(remote(near1.at[side, c], near1.at[side, c], mate))

    def hold_near(side, part_of):
        some_rows = jnp.where(exist(side), near_counts[side, 0:1, :], 0)
        row0 = part_of * half
        value = masked(near1[side, part_of], row0, some_rows, near_counts[side, 1:2, :])
        hold(2 * side, tile_rows(part_of, half), value)

    for side in range(2):
        count_copies[side].wait_recv()
        hold_near(side, c)
    for side in range(2):
        passed[side].wait_recv()
        hold_near(side, 1 - c)
    product(part1)
    full[c, 0] = scatter_sum(part1, sib1, sum1, box1)

    copies = {d: remote(full.at[c, 0], full.at[c, at_slot[n_y - d]], along_y[d]) for d in FAR_FIRST}
    groups, first = [], 0
    for group in NEAR_TO_FAR:
        groups.append((group, pl.ds(first, len(group))))
        first += len(group)
    onward = []
    for group, slots in groups:
        for d in group:
            if d:
                copies[n_y - d].wait_recv()
        here = full.at[c, slots]
        onward.append((
            remote(here, near2.at[0, c, slots], after),
            remote(here, near2.at[1, c, slots], before),
            remote(here, full.at[c, slots], mate),
        ))

    def rows_of(part_of, d):
        return pl.ds(pl.multiple_of(part_of * half + (y + d) % n_y * piece, piece), piece)

    def hold_full(part_of, group):
        for d in group:
            hold(1, rows_of(part_of, d), full[part_of, at_slot[d]])

    for group, slots in groups:
        hold_full(c, group)
    for (group, slots), copy in zip(groups, onward):
        copy[2].wait_recv()
        hold_full(1 - c, group)

    def total_of(term):
        value = None
        for part_of in range(2):
            for d in order:
                add = term(field[rows_of(part_of, d)], full[part_of, at_slot[d]])
                value = add if value is None else value + add
        return jnp.sum(jnp.sum(value, axis=0, keepdims=True), axis=1, keepdims=True)

    square = total_of(lambda f, g: f * f)
    cross = total_of(lambda f, g: f * g)
    own_theta = jnp.where(square > 0, cross / square, 0.0)
    rest = total_of(lambda f, g: (g - own_theta * f) * (g - own_theta * f))
    at = lax.broadcasted_iota(jnp.int32, scal_x.shape[1:], 0)
    scal_x[x] = jnp.where(at == 0, square, jnp.where(at == 1, cross, rest))
    x_copies = [remote(scal_x.at[x], scal_x.at[x], device) for device in along_x]

    def hold_near2(side, part_of, group):
        for d in group:
            value = jnp.where(exist(side), near2[side, part_of, at_slot[d]], 0.0)
            hold(2 * side, rows_of(part_of, d), value)

    passed = []
    for (group, slots), copy in zip(groups, onward):
        for side in range(2):
            copy[side].wait_recv()
            passed.append((side, group, remote(near2.at[side, c, slots], near2.at[side, c, slots], mate)))
    for group, slots in groups:
        for side in range(2):
            hold_near2(side, c, group)
    for copy in x_copies:
        copy.wait_recv()
    scal_z[z] = scal_x[...]
    z_copies = [remote(scal_z.at[z], scal_z.at[z], device) for device in along_z]
    for side, group, copy in passed:
        copy.wait_recv()
        hold_near2(side, 1 - c, group)
    product(part2)
    second = scatter_sum(part2, sib2, sum2, box2)
    for copy in z_copies:
        copy.wait_recv()

    def all_of(i):
        return jnp.concatenate(
            [scal_z[a, b, i:i + 1, :] for a in range(n_z) for b in range(n_x)], axis=0
        )

    squares, crosses, rests = all_of(0), all_of(1), all_of(2)
    thetas = jnp.where(squares > 0, crosses / squares, 0.0)
    theta = jnp.sum(crosses, axis=0, keepdims=True) / jnp.sum(squares, axis=0, keepdims=True)
    gap = (thetas - theta) * jnp.sqrt(squares)
    energy = jnp.sum(rests + gap * gap, axis=0, keepdims=True)
    scale = lax.rsqrt(energy / (n_sec * block * block) + 1e-06)

    last[c, tile_rows(y, piece)] = scale * (second - theta * full[c, 0])
    mine = last.at[c, tile_rows(y, piece)]
    copies = {d: remote(mine, mine, along_y[d]) for d in FAR_FIRST}
    onward = [remote(mine, mine, mate)]
    for d in order[1:]:
        copies[n_y - d].wait_recv()
        here = last.at[c, tile_rows((y + d) % n_y, piece)]
        onward.append(remote(here, here, mate))
    for part_of in range(2):
        for d in order:
            where = rows_of(part_of, d)
            corr[where] = (full[part_of, at_slot[d]] - theta * field[where]) * scale
    image[tile_rows(c, half)] = last[c]
    for copy in onward:
        copy.wait_recv()
    image[tile_rows(1 - c, half)] = last[1 - c]
    for copy in sent:
        copy.wait_send()


def finish_kernel(corr, image, corr_out, image_out, sem):
    copies = [
        pltpu.make_async_copy(corr, corr_out.at[0], sem.at[0]),
        pltpu.make_async_copy(image, image_out.at[0], sem.at[1]),
    ]
    for copy in copies:
        copy.start()
    for copy in copies:
        copy.wait()


def local(n_sec, n_op, state, left, right, shift, rows, cols):
    terms, block = left.shape[0], state.shape[1]
    n_x = min(SEC_X, n_sec)
    n_y = n_op // 2
    half = block // 2
    piece = half // n_y
    f32, bf16 = jnp.float32, jnp.bfloat16
    n_copies = 84
    whole, halves = (block, block), (half, block)
    by_piece = (2, n_y, piece, block)
    in_hbm = [
        pltpu.with_memory_space_constraint(value, pltpu.HBM) for value in (state, left, right, shift)
    ]
    results = pl.pallas_call(
        functools.partial(kernel, (n_sec, n_op, terms, block)),
        out_shape=[pltpu.VMEM(whole, f32)] * 2,
        in_specs=[pl.BlockSpec(memory_space=pltpu.HBM)] * 4 + [pl.BlockSpec(memory_space=pl.ANY)] * 2,
        out_specs=[pl.BlockSpec(memory_space=pltpu.VMEM)] * 2,
        scratch_shapes=[
            pltpu.VMEM(whole, f32),
            pltpu.VMEM((terms,) + whole, f32),
            pltpu.VMEM((terms,) + whole, f32),
            pltpu.SMEM((terms,), jnp.int32),
            pltpu.SMEM((1,), jnp.int32),
            pltpu.SMEM((1,), jnp.int32),
            pltpu.VMEM((2, terms) + whole, bf16),
            pltpu.VMEM((2, terms) + whole, bf16),
            pltpu.VMEM((3, 2) + whole, bf16),
            pltpu.VMEM(whole, f32),
            pltpu.VMEM((2, 2) + halves, f32),
            pltpu.VMEM((2,) + by_piece, f32),
            pltpu.VMEM((2,) + halves, f32),
            pltpu.VMEM((2,) + halves, f32),
            pltpu.VMEM(halves, f32),
            pltpu.VMEM(halves, f32),
            pltpu.VMEM(halves, f32),
            pltpu.VMEM(halves, f32),
            pltpu.VMEM((n_y, piece, block), f32),
            pltpu.VMEM((n_y, piece, block), f32),
            pltpu.VMEM(by_piece, f32),
            pltpu.VMEM((2,) + halves, f32),
            pltpu.VMEM((8, block), jnp.int32),
            pltpu.VMEM((2, 8, block), jnp.int32),
            pltpu.VMEM((n_x, 8, block), f32),
            pltpu.VMEM((n_sec // n_x, n_x, 8, block), f32),
            pltpu.SemaphoreType.DMA((6,)),
            pltpu.SemaphoreType.DMA((n_copies,)),
            pltpu.SemaphoreType.DMA((n_copies,)),
        ],
        compiler_params=pltpu.CompilerParams(
            collective_id=0, has_side_effects=True, vmem_limit_bytes=40 << 20
        ),
        name="davidson",
    )(*in_hbm, rows, cols)
    return pl.pallas_call(
        finish_kernel,
        out_shape=[jax.ShapeDtypeStruct((1,) + whole, f32)] * 2,
        in_specs=[pl.BlockSpec(memory_space=pl.ANY)] * 2,
        out_specs=[pl.BlockSpec(memory_space=pltpu.HBM)] * 2,
        scratch_shapes=[pltpu.SemaphoreType.DMA((2,))],
        name="finish",
    )(*[pltpu.with_memory_space_constraint(value, pltpu.VMEM) for value in results])


def solution(mesh):
    in_specs = (
        P("sec", None, None),
        P("op", "sec", None, None),
        P("op", "sec", None, None),
        P("op"),
        P("sec"),
        P("sec"),
    )
    out_specs = (P("sec", None, None), P("sec", None, None))
    return jax.shard_map(
        functools.partial(local, mesh.shape["sec"], mesh.shape["op"]),
        mesh=mesh, in_specs=in_specs, out_specs=out_specs, check_vma=False,
    )
```

```python
import functools

import jax
import jax.numpy as jnp
from jax import lax
from jax.experimental import pallas as pl
from jax.experimental.pallas import tpu as pltpu
from jax.sharding import PartitionSpec as P

MESH = pl.DeviceIdType.MESH
SEC_X = 4
LANES = 128
HALO_CHUNKS = 2
FAR_FIRST = (4, 3, 5, 2, 6, 1, 7)
NEAR_FIRST = (1, 7, 2, 6, 3, 5, 4)
NN = (((1,), (0,)), ((), ()))
NT = (((1,), (1,)), ((), ()))


def split(value):
    high = value.astype(jnp.bfloat16)
    return high, (value - high.astype(jnp.float32)).astype(jnp.bfloat16)


def dot(a, b, dims):
    return lax.dot_general(a, b, dims, preferred_element_type=jnp.float32)


def dot3(a_high, a_low, b_high, b_low, dims):
    return dot(a_high, b_high, dims) + (dot(a_low, b_high, dims) + dot(a_high, b_low, dims))


def kernel(
    sizes,
    state, left, right, shift, rows, cols,
    corr, image,
    state_v, left_f, right_f, shift_s, rows_s, cols_s,
    left_c, right_c, vec_c,
    field, near1, near2, part1, part2, sib1, sib2, sum1, sum2, box1, box2,
    full, last, counts, near_counts, scal_x, scal_z,
    local_sem, send_sem, recv_sem, line_sem,
):
    n_sec, n_op, terms, block = sizes
    n_x = min(SEC_X, n_sec)
    n_z = n_sec // n_x
    n_y = n_op // 2
    half = block // 2
    piece = half // n_y
    s, o = lax.axis_index("sec"), lax.axis_index("op")
    y, c = lax.div(o, 2), lax.rem(o, 2)
    x, z = lax.rem(s, n_x), lax.div(s, n_x)
    mate = (s, y * 2 + (1 - c))
    after, before = (lax.rem(s + 1, n_sec), o), (lax.rem(s + n_sec - 1, n_sec), o)
    at_y = {0: y, **{d: lax.rem(y + d, n_y) for d in FAR_FIRST}}
    along_y = {d: (s, at_y[d] * 2 + c) for d in FAR_FIRST}
    along_x = [(z * n_x + lax.rem(x + d, n_x), o) for d in range(1, n_x)]
    along_z = [(lax.rem(z + d, n_z) * n_x + x, o) for d in range(1, n_z)]
    rows_of = {d: pl.ds(pl.multiple_of(at_y[d] * piece, piece), piece) for d in at_y}

    count = [0]
    sent = []

    def only(condition, action):
        if condition is None:
            action()
        else:
            pl.when(condition)(action)

    class Remote:
        def __init__(self, src, dst, device, to=None, came=None):
            i = count[0]
            count[0] += 1
            self.to, self.came = to, came
            self.copy = pltpu.make_async_remote_copy(
                src_ref=src, dst_ref=dst, send_sem=send_sem.at[i], recv_sem=recv_sem.at[i],
                device_id=device, device_id_type=MESH,
            )
            only(to, self.copy.start)
            sent.append(self)

        def wait_recv(self):
            only(self.came, self.copy.wait_recv)

        def wait_send(self):
            only(self.to, self.copy.wait_send)

    remote = Remote
    has_before, has_after = s > 0, s < n_sec - 1

    def to_after(src, near):
        return remote(src, near, after, has_after, has_before)

    def to_before(src, near):
        return remote(src, near, before, has_before, has_after)

    def tile_rows(index, size):
        return pl.ds(pl.multiple_of(index * size, size), size)

    def on_line(d):
        return ((z >= d, (s - d * n_x, o)), (z < n_z - d, (s + d * n_x, o)))

    def signal(semaphore, device):
        pl.semaphore_signal(semaphore, inc=1, device_id=device, device_id_type=MESH)

    def greet(semaphore, pairs):
        for condition, device in pairs:
            pl.when(condition)(functools.partial(signal, semaphore, device))

    def heard(pairs):
        return sum(condition.astype(jnp.int32) for condition, _ in pairs)

    always = [mate, *along_y.values(), *along_x]
    sometimes = [(has_after, after), (has_before, before), *on_line(1)]
    barrier = pltpu.get_barrier_semaphore()
    greet(barrier, sometimes)
    for device in always:
        signal(barrier, device)

    def load(i, src, dst):
        copy = pltpu.make_async_copy(src, dst, local_sem.at[i])
        copy.start()
        return copy

    small = [load(0, rows, rows_s), load(1, cols, cols_s), load(2, shift, shift_s)]
    pl.semaphore_wait(barrier, len(always) + heard(sometimes))
    greet(line_sem.at[0], on_line(1))

    chunk = half // HALO_CHUNKS
    chunks = [pl.ds(i * chunk, chunk) for i in range(HALO_CHUNKS)]
    halo = []
    for i, rows_at in enumerate(chunks):
        here = state.at[0, tile_rows(c * HALO_CHUNKS + i, chunk)]
        halo.append((
            to_after(here, near1.at[0, c, rows_at]), to_before(here, near1.at[1, c, rows_at])
        ))
    own_state = load(3, state.at[0], state_v)
    operators = [load(4, left.at[:, 0], left_f), load(5, right.at[:, 0], right_f)]
    for copy in small:
        copy.wait()
    n_rows, n_cols = rows_s[0], cols_s[0]
    at = lax.broadcasted_iota(jnp.int32, counts.shape, 0)
    counts[...] = jnp.where(at == 0, n_rows, n_cols)
    count_copies = [
        to_after(counts, near_counts.at[0]), to_before(counts, near_counts.at[1])
    ]

    def masked(value, row0, some_rows, some_cols):
        at_row = lax.broadcasted_iota(jnp.int32, value.shape, 0) + row0
        at_col = lax.broadcasted_iota(jnp.int32, value.shape, 1)
        return value * ((at_row < some_rows) & (at_col < some_cols)).astype(jnp.float32)

    def hold(slot, where, value):
        high, low = split(value)
        vec_c[slot, 0, where] = high
        vec_c[slot, 1, where] = low

    def product(part):
        total = None
        for k in range(terms):
            source = 1 - shift_s[k]
            inner = dot3(left_c[0, k], left_c[1, k], vec_c[source, 0], vec_c[source, 1], NN)
            high, low = split(inner)
            term = dot3(high, low, right_c[0, k], right_c[1, k], NT)
            total = term if total is None else total + term
        part[0] = total[:half]
        part[1] = total[half:]

    def product_sum(part, sib, summed, box):
        product(part)
        swap = remote(part.at[1 - c], sib, mate)
        swap.wait_recv()
        summed[...] = part[c] + sib[...]
        copies = {}
        for d in FAR_FIRST:
            copies[d] = remote(summed.at[rows_of[d]], box.at[d], along_y[d])
        total = summed[rows_of[0]]
        for d in NEAR_FIRST:
            copies[d].wait_recv()
            total = total + box[d]
        return masked(total, c * half + y * piece, n_rows, n_cols)

    exist = (has_before, has_after)
    for side in range(2):
        @pl.when(jnp.logical_not(exist[side]))
        def _():
            vec_c[2 * side] = jnp.zeros(vec_c.shape[1:], vec_c.dtype)

    own_state.wait()
    field[...] = masked(state_v[...], 0, n_rows, n_cols)
    hold(1, slice(None), field[...])
    for copy in operators:
        copy.wait()
    for k in range(terms):
        left_c[0, k], left_c[1, k] = split(left_f[k])
        right_c[0, k], right_c[1, k] = split(right_f[k])
    pl.semaphore_wait(line_sem.at[0], heard(on_line(1)))
    greet(line_sem.at[1], on_line(2))

    def pass_on(copy, side, here):
        copy.wait_recv()
        return remote(here, here, mate, exist[side], exist[side])

    passed = []
    for rows_at, both in zip(chunks, halo):
        for side in range(2):
            passed.append((side, pass_on(both[side], side, near1.at[side, c, rows_at])))

    def hold_near(side, part_of, i):
        value = masked(
            near1[side, part_of, chunks[i]], part_of * half + i * chunk,
            near_counts[side, 0:1, :], near_counts[side, 1:2, :],
        )
        hold(2 * side, tile_rows(part_of * HALO_CHUNKS + i, chunk), value)

    for side in range(2):
        count_copies[side].wait_recv()
        for i in range(HALO_CHUNKS):
            only(exist[side], functools.partial(hold_near, side, c, i))
    for i, (side, copy) in enumerate(passed):
        copy.wait_recv()
        only(exist[side], functools.partial(hold_near, side, 1 - c, i // 2))
    pl.semaphore_wait(line_sem.at[1], heard(on_line(2)))
    greet(line_sem.at[2], on_line(4))
    full[c, rows_of[0]] = product_sum(part1, sib1, sum1, box1)

    def gather(whole, send_on):
        mine = whole.at[c, rows_of[0]]
        copies = {d: remote(mine, mine, along_y[d]) for d in FAR_FIRST}
        send_on(rows_of[0])
        for d in NEAR_FIRST:
            copies[n_y - d].wait_recv()
            send_on(rows_of[d])

    to_mate, to_near = [], []

    def send_full(at):
        here = full.at[c, at]
        to_near.append((at, 0, to_after(here, near2.at[0, c, at])))
        to_near.append((at, 1, to_before(here, near2.at[1, c, at])))
        to_mate.append(remote(here, here, mate))

    gather(full, send_full)
    hold(1, tile_rows(c, half), full[c])
    for copy in to_mate:
        copy.wait_recv()
    hold(1, tile_rows(1 - c, half), full[1 - c])

    def total_of(term):
        value = term(field[:half], full[0]) + term(field[half:], full[1])
        return jnp.sum(jnp.sum(value, axis=0, keepdims=True), axis=1, keepdims=True)

    square = total_of(lambda f, g: f * f)
    cross = total_of(lambda f, g: f * g)
    own_theta = jnp.where(square > 0, cross / square, 0.0)
    rest = total_of(lambda f, g: (g - own_theta * f) * (g - own_theta * f))
    at = lax.broadcasted_iota(jnp.int32, scal_x.shape[1:], 0)
    scal_x[x] = jnp.where(at == 0, square, jnp.where(at == 1, cross, rest))
    x_copies = [remote(scal_x.at[x], scal_x.at[x], device) for device in along_x]

    def hold_near2(side, part_of):
        hold(2 * side, tile_rows(part_of, half), near2[side, part_of])

    passed = []
    for at, side, copy in to_near:
        passed.append(pass_on(copy, side, near2.at[side, c, at]))
    for side in range(2):
        only(exist[side], functools.partial(hold_near2, side, c))
    for copy in x_copies:
        copy.wait_recv()
    scal_z[z] = scal_x[...]
    pl.semaphore_wait(line_sem.at[2], heard(on_line(4)))
    z_copies = [remote(scal_z.at[z], scal_z.at[z], device) for device in along_z]
    for copy in passed:
        copy.wait_recv()
    for side in range(2):
        only(exist[side], functools.partial(hold_near2, side, 1 - c))
    last[c, rows_of[0]] = product_sum(part2, sib2, sum2, box2)
    to_mate = []

    def send_last(at):
        here = last.at[c, at]
        to_mate.append(remote(here, here, mate))

    gather(last, send_last)
    for copy in z_copies:
        copy.wait_recv()

    def all_of(i):
        return jnp.concatenate(
            [scal_z[a, b, i:i + 1, :] for a in range(n_z) for b in range(n_x)], axis=0
        )

    squares, crosses, rests = all_of(0), all_of(1), all_of(2)
    thetas = jnp.where(squares > 0, crosses / squares, 0.0)
    theta = jnp.sum(crosses, axis=0, keepdims=True) / jnp.sum(squares, axis=0, keepdims=True)
    gap = (thetas - theta) * jnp.sqrt(squares)
    energy = jnp.sum(rests + gap * gap, axis=0, keepdims=True)
    scale = lax.rsqrt(energy / (n_sec * block * block) + 1e-06)

    def finished(part_of):
        image[tile_rows(part_of, half)] = scale * (last[part_of] - theta * full[part_of])

    for part_of in range(2):
        where = slice(part_of * half, (part_of + 1) * half)
        corr[where] = (full[part_of] - theta * field[where]) * scale
    finished(c)
    for copy in to_mate:
        copy.wait_recv()
    finished(1 - c)
    for copy in sent:
        copy.wait_send()


def finish_kernel(corr, image, corr_out, image_out, sem):
    copies = [
        pltpu.make_async_copy(corr, corr_out.at[0], sem.at[0]),
        pltpu.make_async_copy(image, image_out.at[0], sem.at[1]),
    ]
    for copy in copies:
        copy.start()
    for copy in copies:
        copy.wait()


def local(n_sec, n_op, state, left, right, shift, rows, cols):
    terms, block = left.shape[0], state.shape[1]
    n_x = min(SEC_X, n_sec)
    n_y = n_op // 2
    half = block // 2
    piece = half // n_y
    f32, bf16 = jnp.float32, jnp.bfloat16
    n_copies = 128
    whole, halves = (block, block), (half, block)
    in_hbm = [
        pltpu.with_memory_space_constraint(value, pltpu.HBM) for value in (state, left, right, shift)
    ]
    results = pl.pallas_call(
        functools.partial(kernel, (n_sec, n_op, terms, block)),
        out_shape=[pltpu.VMEM(whole, f32)] * 2,
        in_specs=[pl.BlockSpec(memory_space=pltpu.HBM)] * 4 + [pl.BlockSpec(memory_space=pl.ANY)] * 2,
        out_specs=[pl.BlockSpec(memory_space=pltpu.VMEM)] * 2,
        scratch_shapes=[
            pltpu.VMEM(whole, f32),
            pltpu.VMEM((terms,) + whole, f32),
            pltpu.VMEM((terms,) + whole, f32),
            pltpu.SMEM((terms,), jnp.int32),
            pltpu.SMEM((1,), jnp.int32),
            pltpu.SMEM((1,), jnp.int32),
            pltpu.VMEM((2, terms) + whole, bf16),
            pltpu.VMEM((2, terms) + whole, bf16),
            pltpu.VMEM((3, 2) + whole, bf16),
            pltpu.VMEM(whole, f32),
            pltpu.VMEM((2, 2) + halves, f32),
            pltpu.VMEM((2, 2) + halves, f32),
            pltpu.VMEM((2,) + halves, f32),
            pltpu.VMEM((2,) + halves, f32),
            pltpu.VMEM(halves, f32),
            pltpu.VMEM(halves, f32),
            pltpu.VMEM(halves, f32),
            pltpu.VMEM(halves, f32),
            pltpu.VMEM((n_y, piece, block), f32),
            pltpu.VMEM((n_y, piece, block), f32),
            pltpu.VMEM((2,) + halves, f32),
            pltpu.VMEM((2,) + halves, f32),
            pltpu.VMEM((8, block), jnp.int32),
            pltpu.VMEM((2, 8, block), jnp.int32),
            pltpu.VMEM((n_x, 8, block), f32),
            pltpu.VMEM((n_sec // n_x, n_x, 8, block), f32),
            pltpu.SemaphoreType.DMA((6,)),
            pltpu.SemaphoreType.DMA((n_copies,)),
            pltpu.SemaphoreType.DMA((n_copies,)),
            pltpu.SemaphoreType.REGULAR((3,)),
        ],
        compiler_params=pltpu.CompilerParams(
            collective_id=0, has_side_effects=True, vmem_limit_bytes=40 << 20
        ),
        name="davidson",
    )(*in_hbm, rows, cols)
    return pl.pallas_call(
        finish_kernel,
        out_shape=[jax.ShapeDtypeStruct((1,) + whole, f32)] * 2,
        in_specs=[pl.BlockSpec(memory_space=pl.ANY)] * 2,
        out_specs=[pl.BlockSpec(memory_space=pltpu.HBM)] * 2,
        scratch_shapes=[pltpu.SemaphoreType.DMA((2,))],
        name="finish",
    )(*[pltpu.with_memory_space_constraint(value, pltpu.VMEM) for value in results])


def solution(mesh):
    in_specs = (
        P("sec", None, None),
        P("op", "sec", None, None),
        P("op", "sec", None, None),
        P("op"),
        P("sec"),
        P("sec"),
    )
    out_specs = (P("sec", None, None), P("sec", None, None))
    return jax.shard_map(
        functools.partial(local, mesh.shape["sec"], mesh.shape["op"]),
        mesh=mesh, in_specs=in_specs, out_specs=out_specs, check_vma=False,
    )
```

```python
import functools

import jax
import jax.numpy as jnp
from jax import lax
from jax.experimental import pallas as pl
from jax.experimental.pallas import tpu as pltpu
from jax.sharding import PartitionSpec as P

MESH = pl.DeviceIdType.MESH
SEC_X = 4
LANES = 128
HALO_CHUNKS = 2
FAR_FIRST = (4, 3, 5, 2, 6, 1, 7)
NEAR_FIRST = (1, 7, 2, 6, 3, 5, 4)
NN = (((1,), (0,)), ((), ()))
NT = (((1,), (1,)), ((), ()))


def split(value):
    high = value.astype(jnp.bfloat16)
    return high, (value - high.astype(jnp.float32)).astype(jnp.bfloat16)


def dot(a, b, dims):
    return lax.dot_general(a, b, dims, preferred_element_type=jnp.float32)


def dot3(a_high, a_low, b_high, b_low, dims):
    return dot(a_high, b_high, dims) + (dot(a_low, b_high, dims) + dot(a_high, b_low, dims))


def kernel(
    sizes,
    state, left, right, shift, rows, cols,
    corr, image,
    state_v, left_f, right_f, shift_s, rows_s, cols_s,
    left_c, right_c, vec_c,
    field, near1, near2, part1, part2, sib1, sib2, sum1, sum2, box1, box2,
    full, last, counts, near_counts, scal_x, scal_z,
    local_sem, send_sem, recv_sem, line_sem,
):
    n_sec, n_op, terms, block = sizes
    n_x = min(SEC_X, n_sec)
    n_z = n_sec // n_x
    n_y = n_op // 2
    half = block // 2
    piece = half // n_y
    s, o = lax.axis_index("sec"), lax.axis_index("op")
    y, c = lax.div(o, 2), lax.rem(o, 2)
    x, z = lax.rem(s, n_x), lax.div(s, n_x)
    mate = (s, y * 2 + (1 - c))
    after, before = (lax.rem(s + 1, n_sec), o), (lax.rem(s + n_sec - 1, n_sec), o)
    at_y = {0: y, **{d: lax.rem(y + d, n_y) for d in FAR_FIRST}}
    along_y = {d: (s, at_y[d] * 2 + c) for d in FAR_FIRST}
    along_x = [(z * n_x + lax.rem(x + d, n_x), o) for d in range(1, n_x)]
    along_z = [(lax.rem(z + d, n_z) * n_x + x, o) for d in range(1, n_z)]
    rows_of = {d: pl.ds(pl.multiple_of(at_y[d] * piece, piece), piece) for d in at_y}

    count = [0]
    sent = []

    def only(condition, action):
        if condition is None:
            action()
        else:
            pl.when(condition)(action)

    class Remote:
        def __init__(self, src, dst, device, to=None, came=None):
            i = count[0]
            count[0] += 1
            self.to, self.came = to, came
            self.copy = pltpu.make_async_remote_copy(
                src_ref=src, dst_ref=dst, send_sem=send_sem.at[i], recv_sem=recv_sem.at[i],
                device_id=device, device_id_type=MESH,
            )
            only(to, self.copy.start)
            sent.append(self)

        def wait_recv(self):
            only(self.came, self.copy.wait_recv)

        def wait_send(self):
            only(self.to, self.copy.wait_send)

    remote = Remote
    has_before, has_after = s > 0, s < n_sec - 1

    def to_after(src, near):
        return remote(src, near, after, has_after, has_before)

    def to_before(src, near):
        return remote(src, near, before, has_before, has_after)

    def tile_rows(index, size):
        return pl.ds(pl.multiple_of(index * size, size), size)

    def on_line(d):
        return ((z >= d, (s - d * n_x, o)), (z < n_z - d, (s + d * n_x, o)))

    def signal(semaphore, device):
        pl.semaphore_signal(semaphore, inc=1, device_id=device, device_id_type=MESH)

    def greet(semaphore, pairs):
        for condition, device in pairs:
            pl.when(condition)(functools.partial(signal, semaphore, device))

    def heard(pairs):
        return sum(condition.astype(jnp.int32) for condition, _ in pairs)

    always = [mate, *along_y.values(), *along_x]
    sometimes = [(has_after, after), (has_before, before), *on_line(1)]
    barrier = pltpu.get_barrier_semaphore()
    greet(barrier, sometimes)
    for device in always:
        signal(barrier, device)

    def load(i, src, dst):
        copy = pltpu.make_async_copy(src, dst, local_sem.at[i])
        copy.start()
        return copy

    small = [load(0, rows, rows_s), load(1, cols, cols_s), load(2, shift, shift_s)]
    pl.semaphore_wait(barrier, len(always) + heard(sometimes))
    greet(line_sem.at[0], on_line(1))

    chunk = half // HALO_CHUNKS
    chunks = [pl.ds(i * chunk, chunk) for i in range(HALO_CHUNKS)]
    halo = []
    for i, rows_at in enumerate(chunks):
        here = state.at[0, tile_rows(c * HALO_CHUNKS + i, chunk)]
        halo.append((
            to_after(here, near1.at[0, c, rows_at]), to_before(here, near1.at[1, c, rows_at])
        ))
    own_state = load(3, state.at[0], state_v)
    operators = [load(4, left.at[:, 0], left_f), load(5, right.at[:, 0], right_f)]
    for copy in small:
        copy.wait()
    n_rows, n_cols = rows_s[0], cols_s[0]
    at = lax.broadcasted_iota(jnp.int32, counts.shape, 0)
    counts[...] = jnp.where(at == 0, n_rows, n_cols)
    count_copies = [
        to_after(counts, near_counts.at[0]), to_before(counts, near_counts.at[1])
    ]

    def masked(value, row0, some_rows, some_cols):
        at_row = lax.broadcasted_iota(jnp.int32, value.shape, 0) + row0
        at_col = lax.broadcasted_iota(jnp.int32, value.shape, 1)
        return value * ((at_row < some_rows) & (at_col < some_cols)).astype(jnp.float32)

    def hold(slot, where, value):
        high, low = split(value)
        vec_c[slot, 0, where] = high
        vec_c[slot, 1, where] = low

    def product(part):
        total = None
        for k in range(terms):
            source = 1 - shift_s[k]
            inner = dot3(left_c[0, k], left_c[1, k], vec_c[source, 0], vec_c[source, 1], NN)
            high, low = split(inner)
            term = dot3(high, low, right_c[0, k], right_c[1, k], NT)
            total = term if total is None else total + term
        part[0] = total[:half]
        part[1] = total[half:]

    def product_sum(part, sib, summed, box, meanwhile=None):
        product(part)
        swap = remote(part.at[1 - c], sib, mate)
        if meanwhile is not None:
            meanwhile()
        swap.wait_recv()
        summed[...] = part[c] + sib[...]
        copies = {}
        for d in FAR_FIRST:
            copies[d] = remote(summed.at[rows_of[d]], box.at[d], along_y[d])
        total = summed[rows_of[0]]
        for d in NEAR_FIRST:
            copies[d].wait_recv()
            total = total + box[d]
        return masked(total, c * half + y * piece, n_rows, n_cols)

    exist = (has_before, has_after)
    for side in range(2):
        @pl.when(jnp.logical_not(exist[side]))
        def _():
            vec_c[2 * side] = jnp.zeros(vec_c.shape[1:], vec_c.dtype)

    own_state.wait()
    field[...] = masked(state_v[...], 0, n_rows, n_cols)
    hold(1, slice(None), field[...])
    for copy in operators:
        copy.wait()
    for k in range(terms):
        left_c[0, k], left_c[1, k] = split(left_f[k])
        right_c[0, k], right_c[1, k] = split(right_f[k])
    pl.semaphore_wait(line_sem.at[0], heard(on_line(1)))
    greet(line_sem.at[1], on_line(2))

    def pass_on(copy, side, here):
        copy.wait_recv()
        return remote(here, here, mate, exist[side], exist[side])

    passed = []
    for rows_at, both in zip(chunks, halo):
        for side in range(2):
            passed.append((side, pass_on(both[side], side, near1.at[side, c, rows_at])))

    def hold_near(side, part_of, i):
        value = masked(
            near1[side, part_of, chunks[i]], part_of * half + i * chunk,
            near_counts[side, 0:1, :], near_counts[side, 1:2, :],
        )
        hold(2 * side, tile_rows(part_of * HALO_CHUNKS + i, chunk), value)

    for side in range(2):
        count_copies[side].wait_recv()
        for i in range(HALO_CHUNKS):
            only(exist[side], functools.partial(hold_near, side, c, i))
    for i, (side, copy) in enumerate(passed):
        copy.wait_recv()
        only(exist[side], functools.partial(hold_near, side, 1 - c, i // 2))
    pl.semaphore_wait(line_sem.at[1], heard(on_line(2)))
    greet(line_sem.at[2], on_line(4))
    full[c, rows_of[0]] = product_sum(part1, sib1, sum1, box1)

    def gather(whole, send_on):
        mine = whole.at[c, rows_of[0]]
        copies = {d: remote(mine, mine, along_y[d]) for d in FAR_FIRST}
        send_on(rows_of[0])
        for d in NEAR_FIRST:
            copies[n_y - d].wait_recv()
            send_on(rows_of[d])

    to_mate, to_near = [], []

    def send_full(at):
        here = full.at[c, at]
        to_near.append((at, 0, to_after(here, near2.at[0, c, at])))
        to_near.append((at, 1, to_before(here, near2.at[1, c, at])))
        to_mate.append(remote(here, here, mate))

    gather(full, send_full)
    hold(1, tile_rows(c, half), full[c])
    for copy in to_mate:
        copy.wait_recv()
    hold(1, tile_rows(1 - c, half), full[1 - c])

    def total_of(term):
        value = term(field[:half], full[0]) + term(field[half:], full[1])
        return jnp.sum(jnp.sum(value, axis=0, keepdims=True), axis=1, keepdims=True)

    square = total_of(lambda f, g: f * f)
    cross = total_of(lambda f, g: f * g)
    own_theta = jnp.where(square > 0, cross / square, 0.0)
    rest = total_of(lambda f, g: (g - own_theta * f) * (g - own_theta * f))
    at = lax.broadcasted_iota(jnp.int32, scal_x.shape[1:], 0)
    scal_x[x] = jnp.where(at == 0, square, jnp.where(at == 1, cross, rest))
    x_copies = [remote(scal_x.at[x], scal_x.at[x], device) for device in along_x]

    def hold_near2(side, part_of):
        hold(2 * side, tile_rows(part_of, half), near2[side, part_of])

    passed = []
    for at, side, copy in to_near:
        passed.append(pass_on(copy, side, near2.at[side, c, at]))
    for side in range(2):
        only(exist[side], functools.partial(hold_near2, side, c))
    for copy in x_copies:
        copy.wait_recv()
    scal_z[z] = scal_x[...]
    z_copies = []

    def send_scalars():
        pl.semaphore_wait(line_sem.at[2], heard(on_line(4)))
        z_copies.extend(remote(scal_z.at[z], scal_z.at[z], device) for device in along_z)

    for copy in passed:
        copy.wait_recv()
    for side in range(2):
        only(exist[side], functools.partial(hold_near2, side, 1 - c))
    last[c, rows_of[0]] = product_sum(part2, sib2, sum2, box2, send_scalars)
    to_mate = []

    def send_last(at):
        here = last.at[c, at]
        to_mate.append(remote(here, here, mate))

    gather(last, send_last)
    for copy in z_copies:
        copy.wait_recv()

    def all_of(i):
        return jnp.concatenate(
            [scal_z[a, b, i:i + 1, :] for a in range(n_z) for b in range(n_x)], axis=0
        )

    squares, crosses, rests = all_of(0), all_of(1), all_of(2)
    thetas = jnp.where(squares > 0, crosses / squares, 0.0)
    theta = jnp.sum(crosses, axis=0, keepdims=True) / jnp.sum(squares, axis=0, keepdims=True)
    gap = (thetas - theta) * jnp.sqrt(squares)
    energy = jnp.sum(rests + gap * gap, axis=0, keepdims=True)
    scale = lax.rsqrt(energy / (n_sec * block * block) + 1e-06)

    def finished(part_of):
        image[tile_rows(part_of, half)] = scale * (last[part_of] - theta * full[part_of])

    for part_of in range(2):
        where = slice(part_of * half, (part_of + 1) * half)
        corr[where] = (full[part_of] - theta * field[where]) * scale
    finished(c)
    for copy in to_mate:
        copy.wait_recv()
    finished(1 - c)
    for copy in sent:
        copy.wait_send()


def finish_kernel(corr, image, corr_out, image_out, sem):
    copies = [
        pltpu.make_async_copy(corr, corr_out.at[0], sem.at[0]),
        pltpu.make_async_copy(image, image_out.at[0], sem.at[1]),
    ]
    for copy in copies:
        copy.start()
    for copy in copies:
        copy.wait()


def local(n_sec, n_op, state, left, right, shift, rows, cols):
    terms, block = left.shape[0], state.shape[1]
    n_x = min(SEC_X, n_sec)
    n_y = n_op // 2
    half = block // 2
    piece = half // n_y
    f32, bf16 = jnp.float32, jnp.bfloat16
    n_copies = 128
    whole, halves = (block, block), (half, block)
    in_hbm = [
        pltpu.with_memory_space_constraint(value, pltpu.HBM) for value in (state, left, right, shift)
    ]
    results = pl.pallas_call(
        functools.partial(kernel, (n_sec, n_op, terms, block)),
        out_shape=[pltpu.VMEM(whole, f32)] * 2,
        in_specs=[pl.BlockSpec(memory_space=pltpu.HBM)] * 4 + [pl.BlockSpec(memory_space=pl.ANY)] * 2,
        out_specs=[pl.BlockSpec(memory_space=pltpu.VMEM)] * 2,
        scratch_shapes=[
            pltpu.VMEM(whole, f32),
            pltpu.VMEM((terms,) + whole, f32),
            pltpu.VMEM((terms,) + whole, f32),
            pltpu.SMEM((terms,), jnp.int32),
            pltpu.SMEM((1,), jnp.int32),
            pltpu.SMEM((1,), jnp.int32),
            pltpu.VMEM((2, terms) + whole, bf16),
            pltpu.VMEM((2, terms) + whole, bf16),
            pltpu.VMEM((3, 2) + whole, bf16),
            pltpu.VMEM(whole, f32),
            pltpu.VMEM((2, 2) + halves, f32),
            pltpu.VMEM((2, 2) + halves, f32),
            pltpu.VMEM((2,) + halves, f32),
            pltpu.VMEM((2,) + halves, f32),
            pltpu.VMEM(halves, f32),
            pltpu.VMEM(halves, f32),
            pltpu.VMEM(halves, f32),
            pltpu.VMEM(halves, f32),
            pltpu.VMEM((n_y, piece, block), f32),
            pltpu.VMEM((n_y, piece, block), f32),
            pltpu.VMEM((2,) + halves, f32),
            pltpu.VMEM((2,) + halves, f32),
            pltpu.VMEM((8, block), jnp.int32),
            pltpu.VMEM((2, 8, block), jnp.int32),
            pltpu.VMEM((n_x, 8, block), f32),
            pltpu.VMEM((n_sec // n_x, n_x, 8, block), f32),
            pltpu.SemaphoreType.DMA((6,)),
            pltpu.SemaphoreType.DMA((n_copies,)),
            pltpu.SemaphoreType.DMA((n_copies,)),
            pltpu.SemaphoreType.REGULAR((3,)),
        ],
        compiler_params=pltpu.CompilerParams(
            collective_id=0, has_side_effects=True, vmem_limit_bytes=40 << 20
        ),
        name="davidson",
    )(*in_hbm, rows, cols)
    return pl.pallas_call(
        finish_kernel,
        out_shape=[jax.ShapeDtypeStruct((1,) + whole, f32)] * 2,
        in_specs=[pl.BlockSpec(memory_space=pl.ANY)] * 2,
        out_specs=[pl.BlockSpec(memory_space=pltpu.HBM)] * 2,
        scratch_shapes=[pltpu.SemaphoreType.DMA((2,))],
        name="finish",
    )(*[pltpu.with_memory_space_constraint(value, pltpu.VMEM) for value in results])


def solution(mesh):
    in_specs = (
        P("sec", None, None),
        P("op", "sec", None, None),
        P("op", "sec", None, None),
        P("op"),
        P("sec"),
        P("sec"),
    )
    out_specs = (P("sec", None, None), P("sec", None, None))
    return jax.shard_map(
        functools.partial(local, mesh.shape["sec"], mesh.shape["op"]),
        mesh=mesh, in_specs=in_specs, out_specs=out_specs, check_vma=False,
    )
```
